32 devices in a mesh: groups: 2 (over x), tile: 16 (over z, y, core).
Axes of the slice: x: 2, y: 2, z: 4, core: 2. Of those that a mesh axis runs over, the one named last changes fastest.
Arguments:
- latent_rows: bfloat16 [4096, 256], P(('groups', 'tile')), parts along dimension 0, may hold values from -6 to 6
- line_order: int32 [128], P('groups'), parts along dimension 0, may hold values from 0 to 63, each once
- conv_weight: bfloat16 [3, 3, 3, 256, 128], replicated, may hold values from -0.078125 to 0.078125
- conv_bias: float32 [128], replicated, may hold values from -3 to 3
- blend_table: float32 [4, 8], replicated, may hold values from 0.25 to 4
- blend_ids: int32 [32], P('groups'), parts along dimension 0, may hold values from 0 to 3
Outputs:
- frames: bfloat16 [16, 32, 64, 128], P('groups', None, 'tile'), parts along dimension 0
The draws below stay inside these ranges and needn't reach their ends.
There are 2 independent parts, one for each index of `groups`. The reference program is written for one: setup_inputs(seed, part) draws one part's arguments, and reference() takes and returns one part's arrays. A program takes and returns all parts, laid end to end along the dimension named above; an argument that names none is the same for every part. Nothing has to cross between parts.
Inputs may be any that keep to these rules, and one draw needn't show every extreme that they name: line_order is a permutation of the 64 latent lines.
All inputs are finite; a program needn't handle non-finite values.
Results may differ from the reference program's by a relative error of at most 0.001.
Values may be sent and summed in bfloat16 or wider, within the bound.
A program may use at most 64 MiB of HBM per device.

```python
import math
import jax
import jax.numpy as jnp
from jax import lax

CI = 256
CO = 128
LT = 4
LH = 16
WD = 2
KINDS = 4
LINES = 64
WIDTH = 32
TILES = 16
TW = 8
OT = 8
OH = 32


def plant(values, key, least, high):
    index_at = [jax.random.randint(jax.random.fold_in(key, axis), (), 0, length) for axis, length in enumerate(values.shape)]
    widest = values.shape.index(max(values.shape))
    beside = index_at[:widest] + [(index_at[widest] + 1) % values.shape[widest]] + index_at[widest + 1:]
    return values.at[tuple(index_at)].set(least).at[tuple(beside)].set(high)


def level_of(rng, shape, split, low, high):
    level = 1.0
    for position, shards_of in split:
        steps = jax.random.uniform(jax.random.fold_in(jax.random.fold_in(rng, 6), position), (shards_of,), jnp.float32, low / len(split), high / len(split))
        level = level * jnp.repeat(jnp.exp(steps), shape[position] // shards_of).reshape((-1,) + (1,) * (len(shape) - 1 - position))
    return level


def noise(stream_key, extent, spread, limit, cuts=(), held_as=jnp.bfloat16):
    entries = jax.random.normal(stream_key, extent, jnp.float32) * spread
    if len(cuts) > 0:
        entries = level_of(stream_key, extent, cuts, -0.22, 0.18) * entries
    return jnp.clip(entries, min=-limit, max=limit).astype(held_as)


def setup_inputs(seed: int = 0, part: int = 0) -> dict:
    key_list = jax.random.split(jax.random.key(seed), 7)
    part_keys = jax.random.split(jax.random.fold_in(key_list[6], part), 7)
    return {
        "latent_rows": noise(part_keys[0], (LINES * WIDTH, CI), 1.0, 6.0, ((0, 16),)),
        "line_order": jax.random.permutation(part_keys[1], LINES).astype(jnp.int32),
        "conv_weight": noise(key_list[2], (3, 3, 3, CI, CO), (27 * CI) ** -0.5, 0.078125),
        "conv_bias": noise(key_list[3], (CO,), 0.5, 3.0, (), jnp.float32),
        "blend_table": jnp.clip(jnp.exp(jax.random.uniform(key_list[4], (KINDS, TW), jnp.float32, math.log(0.25), math.log(4.0))), 0.25, 4.0),
        "blend_ids": plant(jax.random.randint(part_keys[5], (TILES,), 0, KINDS), jax.random.fold_in(part_keys[5], 1), 0, KINDS - 1).astype(jnp.int32),
    }


def upsample(values):
    values = jnp.repeat(values, 2, axis=0)
    values = jnp.repeat(values, 2, axis=1)
    return jnp.repeat(values, 2, axis=2)


def decode_tile(window, conv_weight, conv_bias):
    upsampled = upsample(window).astype(jnp.float32)
    upsampled = jnp.concatenate([upsampled[:1], upsampled[:1], upsampled], axis=0)
    output = lax.conv_general_dilated(upsampled[None], conv_weight.astype(jnp.float32), (1, 1, 1), [(0, 0), (1, 1), (1, 1)], dimension_numbers=("NDHWC", "DHWIO", "NDHWC"), precision=lax.Precision.HIGHEST)[0]
    return jax.nn.silu(output + conv_bias)


def reference(latent_rows, line_order, conv_weight, conv_bias, blend_table, blend_ids):
    token_rows = latent_rows.reshape(LINES, WIDTH, CI)
    inverse = jnp.zeros((LINES,), jnp.int32).at[line_order].set(jnp.arange(LINES, dtype=jnp.int32))
    latent = token_rows[inverse].reshape(LT, LH, WIDTH, CI)
    padded = jnp.pad(latent, ((0, 0), (0, 0), (1, 1), (0, 0)))
    profiles = blend_table[blend_ids]

    def add_tile(totals, tile_at):
        blended, weight_sum = totals
        window = lax.dynamic_slice_in_dim(padded, tile_at * WD, WD + 2, 2)
        decoded = decode_tile(window, conv_weight, conv_bias)
        profile_row = lax.dynamic_index_in_dim(profiles, tile_at, 0, keepdims=False)
        start = (2 * WD * tile_at).astype(jnp.int32)
        current = lax.dynamic_slice_in_dim(blended, start, TW, 2)
        blended = lax.dynamic_update_slice_in_dim(blended, current + profile_row[None, None, :, None] * decoded, start, 2)
        current_sum = lax.dynamic_slice_in_dim(weight_sum, start, TW, 0)
        weight_sum = lax.dynamic_update_slice_in_dim(weight_sum, current_sum + profile_row, start, 0)
        return (blended, weight_sum), None

    start_totals = (jnp.zeros((OT, OH, 2 * WIDTH + 4, CO), jnp.float32), jnp.zeros((2 * WIDTH + 4,), jnp.float32))
    (blended, weight_sum), unused = lax.scan(add_tile, start_totals, jnp.arange(TILES, dtype=jnp.int32))
    return (blended[:, :, 2:-2] / weight_sum[2:-2][None, None, :, None]).astype(jnp.bfloat16)
```

```python
import functools

import jax
import jax.numpy as jnp
from jax import lax
from jax.experimental import pallas as pl
from jax.experimental.pallas import tpu as pltpu
from jax.sharding import PartitionSpec as P

LT = 4
WD = 2
KW = WD + 2
FIRST = 2
HEAD = 16
F32 = jnp.float32
BF16 = jnp.bfloat16
MESH = pl.DeviceIdType.MESH


def log2(n):
    assert n & (n - 1) == 0
    return n.bit_length() - 1


def iota(shape, dim):
    return lax.broadcasted_iota(jnp.int32, shape, dim)


def dot(a, b):
    return jnp.dot(a, b, preferred_element_type=F32)


def gather_kernel(n, block, lines,
                  rows_hbm, order_hbm, weight_hbm, bias_hbm, table_hbm, ids_hbm,
                  x_ref, weight, params,
                  rows, head, order, bias, table, ids, send, recv,
                  local_sem, head_sem, send_sem, recv_sem, ready_sem):
    me = lax.axis_index("tile")
    lines_dev = lines // n
    width = WD * n
    barrier = pltpu.get_barrier_semaphore()
    heads = [
        pltpu.make_async_copy(
            rows_hbm.at[pl.ds(line * width, HEAD)], head.at[pl.ds(line * HEAD, HEAD)], head_sem.at[line])
        for line in range(lines_dev)
    ]
    loads = [
        pltpu.make_async_copy(source, target, local_sem.at[at])
        for at, (source, target) in enumerate((
            (rows_hbm, rows), (order_hbm, order), (bias_hbm, bias),
            (table_hbm, table), (ids_hbm, ids), (weight_hbm, weight)))
    ]
    for load in heads:
        load.start()
    loads[0].start()

    def enter(j, carry):
        pl.semaphore_signal(barrier, inc=1, device_id={"tile": j}, device_id_type=MESH)
        return carry

    lax.fori_loop(me + 1, n, enter, 0)
    for load in loads[1:]:
        load.start()

    def pick(count, first, pitch):
        shape = (count * block, lines_dev * pitch)
        at = iota(shape, 0)
        inside = at & (block - 1)
        column = (inside >> log2(lines_dev)) + ((at >> log2(block)) + first) * WD - 1
        line = inside & (lines_dev - 1)
        chosen = (iota(shape, 1) == line * pitch + column) & (column >= 0) & (column < width) & (inside < KW * lines_dev)
        return jnp.where(chosen, 1.0, 0.0).astype(BF16)

    def copy_to(peer):
        return pltpu.make_async_remote_copy(
            src_ref=send.at[peer], dst_ref=recv.at[me],
            send_sem=send_sem.at[peer], recv_sem=recv_sem.at[me],
            device_id={"tile": peer}, device_id_type=MESH)

    pick_head = pick(FIRST, 0, HEAD)
    pick_rest = pick(n - FIRST, FIRST, width)
    for load in heads:
        load.wait()
    send[pl.ds(0, FIRST)] = dot(pick_head, head[...]).astype(BF16).reshape(FIRST, block, -1)

    @pl.when(me > 0)
    def _():
        pl.semaphore_wait(barrier, me)

    for j in range(FIRST):
        @pl.when(j < me)
        def _():
            copy_to(j).start()

    def answer(j, carry):
        pl.semaphore_signal(ready_sem.at[me], inc=1, device_id={"tile": j}, device_id_type=MESH)
        return carry

    lax.fori_loop(0, me, answer, 0)

    loads[0].wait()
    send[pl.ds(FIRST, n - FIRST)] = dot(pick_rest, rows[...]).astype(BF16).reshape(n - FIRST, block, -1)
    pltpu.make_async_copy(send.at[me], recv.at[me], recv_sem.at[me]).start()

    def send_lower(j, carry):
        copy_to(j).start()
        return carry

    def send_higher(j, carry):
        pl.semaphore_wait(ready_sem.at[j], 1)
        copy_to(j).start()
        return carry

    lax.fori_loop(FIRST, me, send_lower, 0)
    lax.fori_loop(me + 1, n, send_higher, 0)

    loads[1].wait()
    received = n * block
    shape = (lines, received)
    at = iota(shape, 1)
    inside = at & (block - 1)
    position = (at >> log2(block)) * lines_dev + (inside & (lines_dev - 1))
    expand = jnp.where(iota(shape, 0) == position, 1.0, 0.0).astype(BF16)
    held = jnp.broadcast_to(order[...].astype(F32), (8, lines)).astype(BF16)
    line_of = dot(held, expand)[:1].astype(jnp.int32)
    high = lines // LT
    row = line_of & (high - 1)
    line_of = (line_of - row) * KW + (row & 1) * (high // 2) + (row >> 1)
    inside = iota((1, received), 1) & (block - 1)
    slot = jnp.where(inside < KW * lines_dev, (inside >> log2(lines_dev)) * high + line_of, -1)
    sort = jnp.where(iota((KW * lines, received), 0) == slot, 0.5, 0.0).astype(BF16)

    for load in loads[2:]:
        load.wait()

    def profile(tile):
        kind = ids[tile]
        return [jnp.full((1, 128), table[kind, c], F32) for c in range(4 * WD)]

    has_lower = jnp.where(me > 0, 1.0, 0.0)
    has_upper = jnp.where(me < n - 1, 1.0, 0.0)
    mine = profile(me)[3:-3]
    other = [profile(jnp.maximum(me - 1, 0))[-1] * has_lower, profile(jnp.minimum(me + 1, n - 1))[0] * has_upper]
    for p in range(2):
        total = mine[p] + other[p]
        params[pl.ds(2 * p + 1, 1), :] = mine[p] / total
        params[pl.ds(2 * p + 2, 1), :] = other[p] / total
    params[pl.ds(0, 1), :] = 0.5 * bias[...]

    def sent_to(k, carry):
        copy_to(lax.rem(me + k, n)).wait_send()
        return carry

    lax.fori_loop(1, n, sent_to, 0)

    for j in range(n):
        pltpu.make_async_copy(send.at[j], recv.at[j], recv_sem.at[j]).wait()
    x_ref[...] = dot(sort, recv[...].reshape(received, recv.shape[2])).astype(BF16)


def conv_kernel(lines, x_ref, weight, params, out_hbm, spread, out, sem):
    high = lines // LT
    half = high // 2
    channels = weight.shape[4]
    times, taps_high, taps_wide = weight.shape[:3]

    y = [{} for _ in range(LT)]
    wide = KW * high

    def multiply(frames):
        taps = [(kt, kh) for kh in range(taps_high) for kt in range(times) if kt or frames != (LT - 1,)]
        for at in range(0, len(taps), 2):
            pair = taps[at:at + 2]
            for kw, (first, last) in enumerate(((0, 3), (1, 3), (1, 4))):
                tile = jnp.concatenate([weight[kt, kh, kw] for kt, kh in pair], axis=1)
                rows = [x_ref[pl.ds(f * wide + first * high, (last - first) * high), :] for f in frames]
                product = dot(jnp.concatenate(rows, axis=0), tile)
                for f in frames:
                    for which, (kt, kh) in enumerate(pair):
                        y[f][kt, kh, kw] = {}
                        for column in range(first, last):
                            start = ((f - frames[0]) * (last - first) + column - first) * high
                            y[f][kt, kh, kw][column] = product[start:start + high, which * channels:(which + 1) * channels]

    offset, mine1, other1, mine2, other2 = (params[pl.ds(at, 1), :] for at in range(5))

    def over_time(f, kh, kw, column):
        if f == 0:
            y0, y1, y2 = (y[0][kt, kh, kw][column] for kt in range(times))
            return [(y0 + y1) + y2]
        before0, before1 = (y[f - 1][kt, kh, kw][column] for kt in range(2))
        y1, y2 = (y[f][kt, kh, kw][column] for kt in (1, 2))
        return [(before0 + before1) + y2, before0 + (y1 + y2)]

    def add(*terms):
        return [functools.reduce(lambda a, b: a + b, parts) for parts in zip(*terms)]

    def stages(f):
        stage = []
        for kh in range(taps_high):
            k0 = {column: over_time(f, kh, 0, column) for column in (0, 1, 2)}
            k1 = {column: over_time(f, kh, 1, column) for column in (1, 2)}
            k2 = {column: over_time(f, kh, 2, column) for column in (1, 2, 3)}
            if kh == 1:
                k1 = {column: [v + offset for v in k1[column]] for column in k1}
            lower = add(k0[1], k1[1])
            upper = add(k1[2], k2[2])
            stage.append((
                add(k0[0], k1[1], k2[1]),
                lower, add(lower, k2[2]),
                upper, add(upper, k0[1]),
                add(k0[2], k1[2], k2[3]),
            ))
        return stage

    zero = jnp.zeros((1, channels), F32)

    def act(v):
        return v + v * jnp.tanh(v)

    row_step = 2 * WD
    frame = 2 * high * row_step
    copies = []
    def finish(f):
        stage = stages(f)
        for a in range(len(stage[0][0])):
            g = max(2 * f - 1, 0) + a
            for b in range(2):
                for odd in range(2):
                    d = []
                    for at in range(6):
                        z = [stage[kh][at][a] for kh in range(3)]
                        even0, even1, even2 = (v[:half] for v in z)
                        odd0, odd1, odd2 = (v[half:] for v in z)
                        if b == 0 and odd == 0:
                            v = jnp.concatenate([zero, odd0[:-1]], axis=0) + (even1 + even2)
                        elif b == 0:
                            v = even0 + (odd1 + odd2)
                        elif odd == 0:
                            v = (even0 + even1) + odd2
                        else:
                            v = (odd0 + odd1) + jnp.concatenate([even2[1:], zero], axis=0)
                        d.append(act(v))
                    values = (d[0], mine1 * d[2] + other1 * d[1], mine2 * d[4] + other2 * d[3], d[5])
                    for p, value in enumerate(values):
                        start = g * frame + (2 * odd + b) * row_step + p
                        spread[pl.ds(start, half, stride=4 * row_step), :] = value
            part = pl.ds(g * frame, frame)
            out[part, :] = spread[part, :].astype(BF16)
            for to in (0, 1) if g == 0 else (g + 1,):
                copies.append(pltpu.make_async_copy(out.at[part], out_hbm.at[pl.ds(to * frame, frame)], sem.at[to]))
                copies[-1].start()

    for frames in ((0, 1, 2), (3,)):
        multiply(frames)
        for f in frames:
            finish(f)
    for copy in copies:
        copy.wait()


def per_device(latent_rows, line_order, conv_weight, conv_bias, blend_table, blend_ids):
    n = lax.axis_size("tile")
    lines = line_order.shape[0]
    channels = latent_rows.shape[1]
    out_channels = conv_weight.shape[-1]
    lines_dev = lines // n
    block = 16 * -(-KW * lines_dev // 16)
    frame_rows = 2 * (lines // LT) * 2 * WD
    out_rows = 2 * LT * frame_rows
    hbm = pl.BlockSpec(memory_space=pltpu.HBM)
    vmem = pl.BlockSpec(memory_space=pltpu.VMEM)
    x, weight, params = pl.pallas_call(
        functools.partial(gather_kernel, n, block, lines),
        out_shape=(
            jax.ShapeDtypeStruct((KW * lines, channels), BF16),
            jax.ShapeDtypeStruct(conv_weight.shape, BF16),
            jax.ShapeDtypeStruct((8, out_channels), F32),
        ),
        in_specs=[hbm] * 6,
        out_specs=(vmem,) * 3,
        scratch_shapes=[
            pltpu.VMEM(latent_rows.shape, BF16),
            pltpu.VMEM((lines_dev * HEAD, channels), BF16),
            pltpu.VMEM((1, lines), jnp.int32),
            pltpu.VMEM((1, out_channels), F32),
            pltpu.SMEM(blend_table.shape, F32),
            pltpu.SMEM(blend_ids.shape, jnp.int32),
            pltpu.VMEM((n, block, channels), BF16),
            pltpu.VMEM((n, block, channels), BF16),
            pltpu.SemaphoreType.DMA((6,)),
            pltpu.SemaphoreType.DMA((lines_dev,)),
            pltpu.SemaphoreType.DMA((n,)),
            pltpu.SemaphoreType.DMA((n,)),
            pltpu.SemaphoreType.REGULAR((n,)),
        ],
        compiler_params=pltpu.CompilerParams(collective_id=0, has_side_effects=True, vmem_limit_bytes=20 << 20),
    )(*(pltpu.with_memory_space_constraint(v, pltpu.HBM) for v in (
        latent_rows, line_order.reshape(1, lines), conv_weight,
        conv_bias.reshape(1, out_channels), blend_table, blend_ids)))
    out = pl.pallas_call(
        functools.partial(conv_kernel, lines),
        out_shape=jax.ShapeDtypeStruct((out_rows, out_channels), BF16),
        in_specs=[vmem] * 3,
        out_specs=hbm,
        scratch_shapes=[
            pltpu.VMEM((frame_rows * (2 * LT - 1), out_channels), F32),
            pltpu.VMEM((frame_rows * (2 * LT - 1), out_channels), BF16),
            pltpu.SemaphoreType.DMA((2 * LT,)),
        ],
        compiler_params=pltpu.CompilerParams(vmem_limit_bytes=20 << 20),
    )(x, weight, params)
    return out.reshape(2 * LT, 2 * (lines // LT), 2 * WD, out_channels)


def solution(mesh):
    return jax.shard_map(
        per_device,
        mesh=mesh,
        in_specs=(P(("groups", "tile"), None), P("groups"), P(), P(), P(), P("groups")),
        out_specs=P("groups", None, "tile", None),
        check_vma=False,
    )
```

```python
import functools

import jax
import jax.numpy as jnp
from jax import lax
from jax.experimental import pallas as pl
from jax.experimental.pallas import tpu as pltpu
from jax.sharding import PartitionSpec as P

LT = 4
WD = 2
KW = WD + 2
FIRST = 2
HEAD = 16
F32 = jnp.float32
BF16 = jnp.bfloat16
MESH = pl.DeviceIdType.MESH


def log2(n):
    assert n & (n - 1) == 0
    return n.bit_length() - 1


def iota(shape, dim):
    return lax.broadcasted_iota(jnp.int32, shape, dim)


def dot(a, b):
    return jnp.dot(a, b, preferred_element_type=F32)


def gather_kernel(n, block, lines,
                  rows_hbm, order_hbm, weight_hbm, bias_hbm, table_hbm, ids_hbm,
                  recv, sort, weight, params,
                  rows, head, order, bias, table, ids, send,
                  local_sem, head_sem, send_sem, recv_sem, ready_sem):
    me = lax.axis_index("tile")
    lines_dev = lines // n
    width = WD * n
    barrier = pltpu.get_barrier_semaphore()
    heads = [
        pltpu.make_async_copy(
            rows_hbm.at[pl.ds(line * width, HEAD)], head.at[pl.ds(line * HEAD, HEAD)], head_sem.at[line])
        for line in range(lines_dev)
    ]
    loads = [
        pltpu.make_async_copy(source, target, local_sem.at[at])
        for at, (source, target) in enumerate((
            (rows_hbm, rows), (order_hbm, order), (bias_hbm, bias),
            (table_hbm, table), (ids_hbm, ids), (weight_hbm, weight)))
    ]
    for load in heads:
        load.start()
    loads[0].start()

    def enter(j, carry):
        pl.semaphore_signal(barrier, inc=1, device_id={"tile": j}, device_id_type=MESH)
        return carry

    lax.fori_loop(me + 1, n, enter, 0)
    for load in loads[1:]:
        load.start()

    def pick(count, first, pitch):
        shape = (count * block, lines_dev * pitch)
        at = iota(shape, 0)
        inside = at & (block - 1)
        column = (inside >> log2(lines_dev)) + ((at >> log2(block)) + first) * WD - 1
        line = inside & (lines_dev - 1)
        chosen = (iota(shape, 1) == line * pitch + column) & (column >= 0) & (column < width) & (inside < KW * lines_dev)
        return jnp.where(chosen, 1.0, 0.0).astype(BF16)

    def copy_to(peer):
        return pltpu.make_async_remote_copy(
            src_ref=send.at[peer], dst_ref=recv.at[me],
            send_sem=send_sem.at[peer], recv_sem=recv_sem.at[me],
            device_id={"tile": peer}, device_id_type=MESH)

    pick_head = pick(FIRST, 0, HEAD)
    pick_rest = pick(n - FIRST, FIRST, width)
    for load in heads:
        load.wait()
    send[pl.ds(0, FIRST)] = dot(pick_head, head[...]).astype(BF16).reshape(FIRST, block, -1)

    @pl.when(me > 0)
    def _():
        pl.semaphore_wait(barrier, me)

    for j in range(FIRST):
        @pl.when(j < me)
        def _():
            copy_to(j).start()

    def answer(j, carry):
        pl.semaphore_signal(ready_sem.at[me], inc=1, device_id={"tile": j}, device_id_type=MESH)
        return carry

    lax.fori_loop(0, me, answer, 0)

    loads[0].wait()
    send[pl.ds(FIRST, n - FIRST)] = dot(pick_rest, rows[...]).astype(BF16).reshape(n - FIRST, block, -1)
    pltpu.make_async_copy(send.at[me], recv.at[me], recv_sem.at[me]).start()

    def send_lower(j, carry):
        copy_to(j).start()
        return carry

    def send_higher(j, carry):
        pl.semaphore_wait(ready_sem.at[j], 1)
        copy_to(j).start()
        return carry

    lax.fori_loop(FIRST, me, send_lower, 0)
    lax.fori_loop(me + 1, n, send_higher, 0)

    loads[1].wait()
    received = n * block
    shape = (lines, received)
    at = iota(shape, 1)
    inside = at & (block - 1)
    position = (at >> log2(block)) * lines_dev + (inside & (lines_dev - 1))
    expand = jnp.where(iota(shape, 0) == position, 1.0, 0.0).astype(BF16)
    held = jnp.broadcast_to(order[...].astype(F32), (8, lines)).astype(BF16)
    line_of = dot(held, expand)[:1].astype(jnp.int32)
    high = lines // LT
    row = line_of & (high - 1)
    line_of = (line_of - row) * KW + (row & 1) * (high // 2) + (row >> 1)
    inside = iota((1, received), 1) & (block - 1)
    slot = jnp.where(inside < KW * lines_dev, (inside >> log2(lines_dev)) * high + line_of, -1)
    sort[...] = jnp.where(iota((KW * lines, received), 0) == slot, 0.5, 0.0).astype(BF16)

    for load in loads[2:]:
        load.wait()

    def profile(tile):
        kind = ids[tile]
        return [jnp.full((1, 128), table[kind, c], F32) for c in range(4 * WD)]

    has_lower = jnp.where(me > 0, 1.0, 0.0)
    has_upper = jnp.where(me < n - 1, 1.0, 0.0)
    mine = profile(me)[3:-3]
    other = [profile(jnp.maximum(me - 1, 0))[-1] * has_lower, profile(jnp.minimum(me + 1, n - 1))[0] * has_upper]
    for p in range(2):
        total = mine[p] + other[p]
        params[pl.ds(2 * p + 1, 1), :] = mine[p] / total
        params[pl.ds(2 * p + 2, 1), :] = other[p] / total
    params[pl.ds(0, 1), :] = 0.5 * bias[...]

    def sent_to(k, carry):
        copy_to(lax.rem(me + k, n)).wait_send()
        return carry

    lax.fori_loop(1, n, sent_to, 0)

    for j in range(n):
        pltpu.make_async_copy(send.at[j], recv.at[j], recv_sem.at[j]).wait()


def conv_kernel(lines, recv, sort, weight, params, out_hbm, spread, out, sem):
    x = dot(sort[...], recv[...].reshape(sort.shape[1], recv.shape[2])).astype(BF16)
    high = lines // LT
    half = high // 2
    channels = weight.shape[4]
    times, taps_high, taps_wide = weight.shape[:3]

    y = [{} for _ in range(LT)]
    wide = KW * high

    def multiply(frames, highs):
        taps = [(kt, kh) for kh in highs for kt in range(times) if kt or frames != (LT - 1,)]
        for at in range(0, len(taps), 2):
            pair = taps[at:at + 2]
            for kw, (first, last) in enumerate(((0, 3), (1, 3), (1, 4))):
                tile = jnp.concatenate([weight[kt, kh, kw] for kt, kh in pair], axis=1)
                rows = [x[f * wide + first * high:f * wide + last * high] for f in frames]
                product = dot(jnp.concatenate(rows, axis=0), tile)
                for f in frames:
                    for which, (kt, kh) in enumerate(pair):
                        y[f][kt, kh, kw] = {}
                        for column in range(first, last):
                            start = ((f - frames[0]) * (last - first) + column - first) * high
                            y[f][kt, kh, kw][column] = product[start:start + high, which * channels:(which + 1) * channels]

    offset, mine1, other1, mine2, other2 = (params[pl.ds(at, 1), :] for at in range(5))

    def over_time(f, kh, kw, column):
        if f == 0:
            y0, y1, y2 = (y[0][kt, kh, kw][column] for kt in range(times))
            return [(y0 + y1) + y2]
        before0, before1 = (y[f - 1][kt, kh, kw][column] for kt in range(2))
        y1, y2 = (y[f][kt, kh, kw][column] for kt in (1, 2))
        return [(before0 + before1) + y2, before0 + (y1 + y2)]

    def add(*terms):
        return [functools.reduce(lambda a, b: a + b, parts) for parts in zip(*terms)]

    def stages(f):
        stage = []
        for kh in range(taps_high):
            k0 = {column: over_time(f, kh, 0, column) for column in (0, 1, 2)}
            k1 = {column: over_time(f, kh, 1, column) for column in (1, 2)}
            k2 = {column: over_time(f, kh, 2, column) for column in (1, 2, 3)}
            if kh == 1:
                k1 = {column: [v + offset for v in k1[column]] for column in k1}
            lower = add(k0[1], k1[1])
            upper = add(k1[2], k2[2])
            stage.append((
                add(k0[0], k1[1], k2[1]),
                lower, add(lower, k2[2]),
                upper, add(upper, k0[1]),
                add(k0[2], k1[2], k2[3]),
            ))
        return stage

    zero = jnp.zeros((1, channels), F32)

    def act(v):
        return v + v * jnp.tanh(v)

    row_step = 2 * WD
    frame = 2 * high * row_step
    copies = []
    def finish(f):
        stage = stages(f)
        for a in range(len(stage[0][0])):
            g = max(2 * f - 1, 0) + a
            for b in range(2):
                for odd in range(2):
                    d = []
                    for at in range(6):
                        z = [stage[kh][at][a] for kh in range(3)]
                        even0, even1, even2 = (v[:half] for v in z)
                        odd0, odd1, odd2 = (v[half:] for v in z)
                        if b == 0 and odd == 0:
                            v = (jnp.concatenate([zero, odd0[:-1]], axis=0) + even1) + even2
                        elif b == 0:
                            v = (even0 + odd1) + odd2
                        elif odd == 0:
                            v = (even0 + even1) + odd2
                        else:
                            v = (odd0 + odd1) + jnp.concatenate([even2[1:], zero], axis=0)
                        d.append(act(v))
                    values = (d[0], mine1 * d[2] + other1 * d[1], mine2 * d[4] + other2 * d[3], d[5])
                    for p, value in enumerate(values):
                        start = g * frame + (2 * odd + b) * row_step + p
                        spread[pl.ds(start, half, stride=4 * row_step), :] = value
            part = pl.ds(g * frame, frame)
            out[part, :] = spread[part, :].astype(BF16)
            for to in (0, 1) if g == 0 else (g + 1,):
                copies.append(pltpu.make_async_copy(out.at[part], out_hbm.at[pl.ds(to * frame, frame)], sem.at[to]))
                copies[-1].start()

    multiply(tuple(range(LT)), (0, 1))
    for frames in ((0, 1, 2), (3,)):
        multiply(frames, (2,))
        for f in frames:
            finish(f)
    for copy in copies:
        copy.wait()


def per_device(latent_rows, line_order, conv_weight, conv_bias, blend_table, blend_ids):
    n = lax.axis_size("tile")
    lines = line_order.shape[0]
    channels = latent_rows.shape[1]
    out_channels = conv_weight.shape[-1]
    lines_dev = lines // n
    block = 16 * -(-KW * lines_dev // 16)
    frame_rows = 2 * (lines // LT) * 2 * WD
    out_rows = 2 * LT * frame_rows
    hbm = pl.BlockSpec(memory_space=pltpu.HBM)
    vmem = pl.BlockSpec(memory_space=pltpu.VMEM)
    gathered = pl.pallas_call(
        functools.partial(gather_kernel, n, block, lines),
        out_shape=(
            jax.ShapeDtypeStruct((n, block, channels), BF16),
            jax.ShapeDtypeStruct((KW * lines, n * block), BF16),
            jax.ShapeDtypeStruct(conv_weight.shape, BF16),
            jax.ShapeDtypeStruct((8, out_channels), F32),
        ),
        in_specs=[hbm] * 6,
        out_specs=(vmem,) * 4,
        scratch_shapes=[
            pltpu.VMEM(latent_rows.shape, BF16),
            pltpu.VMEM((lines_dev * HEAD, channels), BF16),
            pltpu.VMEM((1, lines), jnp.int32),
            pltpu.VMEM((1, out_channels), F32),
            pltpu.SMEM(blend_table.shape, F32),
            pltpu.SMEM(blend_ids.shape, jnp.int32),
            pltpu.VMEM((n, block, channels), BF16),
            pltpu.SemaphoreType.DMA((6,)),
            pltpu.SemaphoreType.DMA((lines_dev,)),
            pltpu.SemaphoreType.DMA((n,)),
            pltpu.SemaphoreType.DMA((n,)),
            pltpu.SemaphoreType.REGULAR((n,)),
        ],
        compiler_params=pltpu.CompilerParams(collective_id=0, has_side_effects=True, vmem_limit_bytes=20 << 20),
    )(*(pltpu.with_memory_space_constraint(v, pltpu.HBM) for v in (
        latent_rows, line_order.reshape(1, lines), conv_weight,
        conv_bias.reshape(1, out_channels), blend_table, blend_ids)))
    out = pl.pallas_call(
        functools.partial(conv_kernel, lines),
        out_shape=jax.ShapeDtypeStruct((out_rows, out_channels), BF16),
        in_specs=[vmem] * 4,
        out_specs=hbm,
        scratch_shapes=[
            pltpu.VMEM((frame_rows * (2 * LT - 1), out_channels), F32),
            pltpu.VMEM((frame_rows * (2 * LT - 1), out_channels), BF16),
            pltpu.SemaphoreType.DMA((2 * LT,)),
        ],
        compiler_params=pltpu.CompilerParams(vmem_limit_bytes=20 << 20),
    )(*gathered)
    return out.reshape(2 * LT, 2 * (lines // LT), 2 * WD, out_channels)


def solution(mesh):
    return jax.shard_map(
        per_device,
        mesh=mesh,
        in_specs=(P(("groups", "tile"), None), P("groups"), P(), P(), P(), P("groups")),
        out_specs=P("groups", None, "tile", None),
        check_vma=False,
    )
```

```python
import functools

import jax
import jax.numpy as jnp
from jax import lax
from jax.experimental import pallas as pl
from jax.experimental.pallas import tpu as pltpu
from jax.sharding import PartitionSpec as P

LT = 4
WD = 2
KW = WD + 2
FIRST = 2
HEAD = 16
F32 = jnp.float32
BF16 = jnp.bfloat16
MESH = pl.DeviceIdType.MESH


def log2(n):
    assert n & (n - 1) == 0
    return n.bit_length() - 1


def iota(shape, dim):
    return lax.broadcasted_iota(jnp.int32, shape, dim)


def dot(a, b):
    return jnp.dot(a, b, preferred_element_type=F32)


def gather_kernel(n, block, lines,
                  rows_hbm, order_hbm, weight_hbm, bias_hbm, table_hbm, ids_hbm,
                  recv, sort, weight, params,
                  rows, head, order, bias, table, ids, send,
                  local_sem, head_sem, send_sem, recv_sem, ready_sem):
    me = lax.axis_index("tile")
    lines_dev = lines // n
    width = WD * n
    barrier = pltpu.get_barrier_semaphore()
    heads = [
        pltpu.make_async_copy(
            rows_hbm.at[pl.ds(line * width, HEAD)], head.at[pl.ds(line * HEAD, HEAD)], head_sem.at[line])
        for line in range(lines_dev)
    ]
    loads = [
        pltpu.make_async_copy(source, target, local_sem.at[at])
        for at, (source, target) in enumerate((
            (rows_hbm, rows), (order_hbm, order), (bias_hbm, bias),
            (table_hbm, table), (ids_hbm, ids), (weight_hbm, weight)))
    ]
    for load in heads:
        load.start()
    loads[0].start()

    def enter(j, carry):
        pl.semaphore_signal(barrier, inc=1, device_id={"tile": j}, device_id_type=MESH)
        return carry

    lax.fori_loop(me + 1, n, enter, 0)
    for load in loads[1:]:
        load.start()

    def pick(count, first, pitch):
        shape = (count * block, lines_dev * pitch)
        at = iota(shape, 0)
        inside = at & (block - 1)
        column = (inside >> log2(lines_dev)) + ((at >> log2(block)) + first) * WD - 1
        line = inside & (lines_dev - 1)
        chosen = (iota(shape, 1) == line * pitch + column) & (column >= 0) & (column < width) & (inside < KW * lines_dev)
        return jnp.where(chosen, 1.0, 0.0).astype(BF16)

    def copy_to(peer):
        return pltpu.make_async_remote_copy(
            src_ref=send.at[peer], dst_ref=recv.at[me],
            send_sem=send_sem.at[peer], recv_sem=recv_sem.at[me],
            device_id={"tile": peer}, device_id_type=MESH)

    pick_head = pick(FIRST - 1, 1, HEAD)
    pick_rest = pick(n - FIRST, FIRST, width)
    for load in heads:
        load.wait()
    near = head[...].astype(F32)
    pieces = [near[line * HEAD:line * HEAD + KW] for line in range(lines_dev)]
    if block > KW * lines_dev:
        pieces.append(jnp.zeros((block - KW * lines_dev, near.shape[1]), F32))
    send[0] = jnp.concatenate(pieces, axis=0).astype(BF16)

    @pl.when(me > 0)
    def _():
        pl.semaphore_wait(barrier, me)
        copy_to(0).start()

    send[pl.ds(1, FIRST - 1)] = dot(pick_head, head[...]).astype(BF16).reshape(FIRST - 1, block, -1)
    for j in range(1, FIRST):
        @pl.when(j < me)
        def _():
            copy_to(j).start()

    def answer(j, carry):
        pl.semaphore_signal(ready_sem.at[me], inc=1, device_id={"tile": j}, device_id_type=MESH)
        return carry

    lax.fori_loop(0, me, answer, 0)

    loads[0].wait()
    send[pl.ds(FIRST, n - FIRST)] = dot(pick_rest, rows[...]).astype(BF16).reshape(n - FIRST, block, -1)
    pltpu.make_async_copy(send.at[me], recv.at[me], recv_sem.at[me]).start()

    def send_lower(j, carry):
        copy_to(j).start()
        return carry

    def send_higher(j, carry):
        pl.semaphore_wait(ready_sem.at[j], 1)
        copy_to(j).start()
        return carry

    lax.fori_loop(FIRST, me, send_lower, 0)
    lax.fori_loop(me + 1, n, send_higher, 0)

    loads[1].wait()
    received = n * block

    def entry(shape, dim):
        at = iota(shape, dim)
        inside = at & (block - 1)
        by_line = me == 0
        line = jnp.where(by_line, inside >> log2(KW), inside & (lines_dev - 1))
        column = jnp.where(by_line, (inside & (KW - 1)) + 1, inside >> log2(lines_dev))
        valid = (inside < KW * lines_dev) & (column < KW)
        return (at >> log2(block)) * lines_dev + line, column, valid

    shape = (lines, received)
    position, _, valid = entry(shape, 1)
    expand = jnp.where((iota(shape, 0) == position) & valid, 1.0, 0.0).astype(BF16)
    held = jnp.broadcast_to(order[...].astype(F32), (8, lines)).astype(BF16)
    line_of = dot(held, expand)[:1].astype(jnp.int32)
    high = lines // LT
    row = line_of & (high - 1)
    line_of = (line_of - row) * KW + (row & 1) * (high // 2) + (row >> 1)
    _, column, valid = entry((1, received), 1)
    slot = jnp.where(valid, column * high + line_of, -1)
    sort[...] = jnp.where(iota((KW * lines, received), 0) == slot, 0.5, 0.0).astype(BF16)

    for load in loads[2:]:
        load.wait()

    def profile(tile):
        kind = ids[tile]
        return [jnp.full((1, 128), table[kind, c], F32) for c in range(4 * WD)]

    has_lower = jnp.where(me > 0, 1.0, 0.0)
    has_upper = jnp.where(me < n - 1, 1.0, 0.0)
    mine = profile(me)[3:-3]
    other = [profile(jnp.maximum(me - 1, 0))[-1] * has_lower, profile(jnp.minimum(me + 1, n - 1))[0] * has_upper]
    for p in range(2):
        total = mine[p] + other[p]
        params[pl.ds(2 * p + 1, 1), :] = mine[p] / total
        params[pl.ds(2 * p + 2, 1), :] = other[p] / total
    params[pl.ds(0, 1), :] = 0.5 * bias[...]

    def sent_to(k, carry):
        copy_to(lax.rem(me + k, n)).wait_send()
        return carry

    lax.fori_loop(1, n, sent_to, 0)

    for j in range(n):
        pltpu.make_async_copy(send.at[j], recv.at[j], recv_sem.at[j]).wait()


def conv_kernel(lines, recv, sort, weight, params, out_hbm, spread, out, sem):
    x = dot(sort[...], recv[...].reshape(sort.shape[1], recv.shape[2])).astype(BF16)
    high = lines // LT
    half = high // 2
    channels = weight.shape[4]
    times, taps_high, taps_wide = weight.shape[:3]

    y = [{} for _ in range(LT)]
    wide = KW * high

    def multiply(frames, highs):
        taps = [(kt, kh) for kh in highs for kt in range(times) if kt or frames != (LT - 1,)]
        for at in range(0, len(taps), 2):
            pair = taps[at:at + 2]
            for kw, (first, last) in enumerate(((0, 3), (1, 3), (1, 4))):
                tile = jnp.concatenate([weight[kt, kh, kw] for kt, kh in pair], axis=1)
                rows = [x[f * wide + first * high:f * wide + last * high] for f in frames]
                product = dot(jnp.concatenate(rows, axis=0), tile)
                for f in frames:
                    for which, (kt, kh) in enumerate(pair):
                        y[f][kt, kh, kw] = {}
                        for column in range(first, last):
                            start = ((f - frames[0]) * (last - first) + column - first) * high
                            y[f][kt, kh, kw][column] = product[start:start + high, which * channels:(which + 1) * channels]

    offset, mine1, other1, mine2, other2 = (params[pl.ds(at, 1), :] for at in range(5))

    def over_time(f, kh, kw, column):
        if f == 0:
            y0, y1, y2 = (y[0][kt, kh, kw][column] for kt in range(times))
            return [(y0 + y1) + y2]
        before0, before1 = (y[f - 1][kt, kh, kw][column] for kt in range(2))
        y1, y2 = (y[f][kt, kh, kw][column] for kt in (1, 2))
        return [(before0 + before1) + y2, before0 + (y1 + y2)]

    def add(*terms):
        return [functools.reduce(lambda a, b: a + b, parts) for parts in zip(*terms)]

    def stages(f):
        stage = []
        for kh in range(taps_high):
            k0 = {column: over_time(f, kh, 0, column) for column in (0, 1, 2)}
            k1 = {column: over_time(f, kh, 1, column) for column in (1, 2)}
            k2 = {column: over_time(f, kh, 2, column) for column in (1, 2, 3)}
            if kh == 1:
                k1 = {column: [v + offset for v in k1[column]] for column in k1}
            lower = add(k0[1], k1[1])
            upper = add(k1[2], k2[2])
            stage.append((
                add(k0[0], k1[1], k2[1]),
                lower, add(lower, k2[2]),
                upper, add(upper, k0[1]),
                add(k0[2], k1[2], k2[3]),
            ))
        return stage

    zero = jnp.zeros((1, channels), F32)

    def act(v):
        return v + v * jnp.tanh(v)

    row_step = 2 * WD
    frame = 2 * high * row_step
    copies = []
    def finish(f):
        stage = stages(f)
        for a in range(len(stage[0][0])):
            g = max(2 * f - 1, 0) + a
            for b in range(2):
                for odd in range(2):
                    d = []
                    for at in range(6):
                        z = [stage[kh][at][a] for kh in range(3)]
                        even0, even1, even2 = (v[:half] for v in z)
                        odd0, odd1, odd2 = (v[half:] for v in z)
                        if b == 0 and odd == 0:
                            v = (jnp.concatenate([zero, odd0[:-1]], axis=0) + even1) + even2
                        elif b == 0:
                            v = (even0 + odd1) + odd2
                        elif odd == 0:
                            v = (even0 + even1) + odd2
                        else:
                            v = (odd0 + odd1) + jnp.concatenate([even2[1:], zero], axis=0)
                        d.append(act(v))
                    values = (d[0], mine1 * d[2] + other1 * d[1], mine2 * d[4] + other2 * d[3], d[5])
                    for p, value in enumerate(values):
                        start = g * frame + (2 * odd + b) * row_step + p
                        spread[pl.ds(start, half, stride=4 * row_step), :] = value
            part = pl.ds(g * frame, frame)
            out[part, :] = spread[part, :].astype(BF16)
            for to in (0, 1) if g == 0 else (g + 1,):
                copies.append(pltpu.make_async_copy(out.at[part], out_hbm.at[pl.ds(to * frame, frame)], sem.at[to]))
                copies[-1].start()

    multiply(tuple(range(LT)), (0, 1))
    for frames in ((0, 1, 2), (3,)):
        multiply(frames, (2,))
        for f in frames:
            finish(f)
    for copy in copies:
        copy.wait()


def per_device(latent_rows, line_order, conv_weight, conv_bias, blend_table, blend_ids):
    n = lax.axis_size("tile")
    lines = line_order.shape[0]
    channels = latent_rows.shape[1]
    out_channels = conv_weight.shape[-1]
    lines_dev = lines // n
    block = 16 * -(-KW * lines_dev // 16)
    frame_rows = 2 * (lines // LT) * 2 * WD
    out_rows = 2 * LT * frame_rows
    hbm = pl.BlockSpec(memory_space=pltpu.HBM)
    vmem = pl.BlockSpec(memory_space=pltpu.VMEM)
    gathered = pl.pallas_call(
        functools.partial(gather_kernel, n, block, lines),
        out_shape=(
            jax.ShapeDtypeStruct((n, block, channels), BF16),
            jax.ShapeDtypeStruct((KW * lines, n * block), BF16),
            jax.ShapeDtypeStruct(conv_weight.shape, BF16),
            jax.ShapeDtypeStruct((8, out_channels), F32),
        ),
        in_specs=[hbm] * 6,
        out_specs=(vmem,) * 4,
        scratch_shapes=[
            pltpu.VMEM(latent_rows.shape, BF16),
            pltpu.VMEM((lines_dev * HEAD, channels), BF16),
            pltpu.VMEM((1, lines), jnp.int32),
            pltpu.VMEM((1, out_channels), F32),
            pltpu.SMEM(blend_table.shape, F32),
            pltpu.SMEM(blend_ids.shape, jnp.int32),
            pltpu.VMEM((n, block, channels), BF16),
            pltpu.SemaphoreType.DMA((6,)),
            pltpu.SemaphoreType.DMA((lines_dev,)),
            pltpu.SemaphoreType.DMA((n,)),
            pltpu.SemaphoreType.DMA((n,)),
            pltpu.SemaphoreType.REGULAR((n,)),
        ],
        compiler_params=pltpu.CompilerParams(collective_id=0, has_side_effects=True, vmem_limit_bytes=20 << 20),
    )(*(pltpu.with_memory_space_constraint(v, pltpu.HBM) for v in (
        latent_rows, line_order.reshape(1, lines), conv_weight,
        conv_bias.reshape(1, out_channels), blend_table, blend_ids)))
    out = pl.pallas_call(
        functools.partial(conv_kernel, lines),
        out_shape=jax.ShapeDtypeStruct((out_rows, out_channels), BF16),
        in_specs=[vmem] * 4,
        out_specs=hbm,
        scratch_shapes=[
            pltpu.VMEM((frame_rows * (2 * LT - 1), out_channels), F32),
            pltpu.VMEM((frame_rows * (2 * LT - 1), out_channels), BF16),
            pltpu.SemaphoreType.DMA((2 * LT,)),
        ],
        compiler_params=pltpu.CompilerParams(vmem_limit_bytes=20 << 20),
    )(*gathered)
    return out.reshape(2 * LT, 2 * (lines // LT), 2 * WD, out_channels)


def solution(mesh):
    return jax.shard_map(
        per_device,
        mesh=mesh,
        in_specs=(P(("groups", "tile"), None), P("groups"), P(), P(), P(), P("groups")),
        out_specs=P("groups", None, "tile", None),
        check_vma=False,
    )
```

```python
import functools

import jax
import jax.numpy as jnp
from jax import lax
from jax.experimental import pallas as pl
from jax.experimental.pallas import tpu as pltpu
from jax.sharding import PartitionSpec as P

LT = 4
WD = 2
KW = WD + 2
FIRST = 2
HEAD = 16
F32 = jnp.float32
BF16 = jnp.bfloat16
MESH = pl.DeviceIdType.MESH


def log2(n):
    assert n & (n - 1) == 0
    return n.bit_length() - 1


def iota(shape, dim):
    return lax.broadcasted_iota(jnp.int32, shape, dim)


def dot(a, b):
    return jnp.dot(a, b, preferred_element_type=F32)


def gather_kernel(n, block, lines,
                  rows_hbm, order_hbm, weight_hbm, bias_hbm, table_hbm, ids_hbm,
                  recv, sort, weight, params,
                  rows, head, order, bias, table, ids, send,
                  local_sem, head_sem, send_sem, recv_sem, ready_sem):
    me = lax.axis_index("tile")
    lines_dev = lines // n
    width = WD * n
    barrier = pltpu.get_barrier_semaphore()
    heads = [
        pltpu.make_async_copy(
            rows_hbm.at[pl.ds(line * width, HEAD)], head.at[pl.ds(line * HEAD, HEAD)], head_sem.at[line])
        for line in range(lines_dev)
    ]
    loads = [
        pltpu.make_async_copy(source, target, local_sem.at[at])
        for at, (source, target) in enumerate((
            (rows_hbm, rows), (order_hbm, order), (bias_hbm, bias),
            (table_hbm, table), (ids_hbm, ids), (weight_hbm, weight)))
    ]
    for load in heads:
        load.start()
    loads[0].start()

    def enter(j, carry):
        pl.semaphore_signal(barrier, inc=1, device_id={"tile": j}, device_id_type=MESH)
        return carry

    lax.fori_loop(me + 1, n, enter, 0)
    for load in loads[1:]:
        load.start()

    def pick(count, first, pitch):
        shape = (count * block, lines_dev * pitch)
        at = iota(shape, 0)
        inside = at & (block - 1)
        column = (inside >> log2(lines_dev)) + ((at >> log2(block)) + first) * WD - 1
        line = inside & (lines_dev - 1)
        chosen = (iota(shape, 1) == line * pitch + column) & (column >= 0) & (column < width) & (inside < KW * lines_dev)
        return jnp.where(chosen, 1.0, 0.0).astype(BF16)

    def copy_to(peer):
        return pltpu.make_async_remote_copy(
            src_ref=send.at[peer], dst_ref=recv.at[me],
            send_sem=send_sem.at[peer], recv_sem=recv_sem.at[me],
            device_id={"tile": peer}, device_id_type=MESH)

    pick_head = pick(FIRST - 1, 1, HEAD)
    pick_rest = pick(n - FIRST, FIRST, width)
    def answer(j, carry):
        pl.semaphore_signal(ready_sem.at[me], inc=1, device_id={"tile": j}, device_id_type=MESH)
        return carry

    @pl.when(me > 0)
    def _():
        pl.semaphore_wait(barrier, me)
        answer(0, 0)

    for load in heads:
        load.wait()
    near = head[...].astype(F32)
    pieces = [near[line * HEAD:line * HEAD + KW] for line in range(lines_dev)]
    if block > KW * lines_dev:
        pieces.append(jnp.zeros((block - KW * lines_dev, near.shape[1]), F32))
    send[0] = jnp.concatenate(pieces, axis=0).astype(BF16)

    @pl.when(me > 0)
    def _():
        copy_to(0).start()

    send[pl.ds(1, FIRST - 1)] = dot(pick_head, head[...]).astype(BF16).reshape(FIRST - 1, block, -1)
    for j in range(1, FIRST):
        @pl.when(j < me)
        def _():
            copy_to(j).start()

    lax.fori_loop(1, me, answer, 0)

    loads[0].wait()
    send[pl.ds(FIRST, n - FIRST)] = dot(pick_rest, rows[...]).astype(BF16).reshape(n - FIRST, block, -1)
    pltpu.make_async_copy(send.at[me], recv.at[me], recv_sem.at[me]).start()

    def send_lower(j, carry):
        copy_to(j).start()
        return carry

    def send_higher(j, carry):
        pl.semaphore_wait(ready_sem.at[j], 1)
        copy_to(j).start()
        return carry

    lax.fori_loop(FIRST, me, send_lower, 0)
    lax.fori_loop(me + 1, n, send_higher, 0)

    loads[1].wait()
    received = n * block

    def entry(shape, dim):
        at = iota(shape, dim)
        inside = at & (block - 1)
        by_line = me == 0
        line = jnp.where(by_line, inside >> log2(KW), inside & (lines_dev - 1))
        column = jnp.where(by_line, (inside & (KW - 1)) + 1, inside >> log2(lines_dev))
        valid = (inside < KW * lines_dev) & (column < KW)
        return (at >> log2(block)) * lines_dev + line, column, valid

    shape = (lines, received)
    position, _, valid = entry(shape, 1)
    expand = jnp.where((iota(shape, 0) == position) & valid, 1.0, 0.0).astype(BF16)
    held = jnp.broadcast_to(order[...].astype(F32), (8, lines)).astype(BF16)
    line_of = dot(held, expand)[:1].astype(jnp.int32)
    high = lines // LT
    row = line_of & (high - 1)
    line_of = (line_of - row) * KW + (row & 1) * (high // 2) + (row >> 1)
    _, column, valid = entry((1, received), 1)
    slot = jnp.where(valid, column * high + line_of, -1)
    sort[...] = jnp.where(iota((KW * lines, received), 0) == slot, 0.5, 0.0).astype(BF16)

    for load in loads[2:]:
        load.wait()

    def profile(tile):
        kind = ids[tile]
        return [jnp.full((1, 128), table[kind, c], F32) for c in range(4 * WD)]

    has_lower = jnp.where(me > 0, 1.0, 0.0)
    has_upper = jnp.where(me < n - 1, 1.0, 0.0)
    mine = profile(me)[3:-3]
    other = [profile(jnp.maximum(me - 1, 0))[-1] * has_lower, profile(jnp.minimum(me + 1, n - 1))[0] * has_upper]
    for p in range(2):
        total = mine[p] + other[p]
        params[pl.ds(2 * p + 1, 1), :] = mine[p] / total
        params[pl.ds(2 * p + 2, 1), :] = other[p] / total
    params[pl.ds(0, 1), :] = 0.5 * bias[...]

    def sent_to(k, carry):
        copy_to(lax.rem(me + k, n)).wait_send()
        return carry

    lax.fori_loop(1, n, sent_to, 0)

    for j in range(n):
        pltpu.make_async_copy(send.at[j], recv.at[j], recv_sem.at[j]).wait()


def conv_kernel(lines, recv, sort, weight, params, out_hbm, spread, out, sem):
    x = dot(sort[...], recv[...].reshape(sort.shape[1], recv.shape[2])).astype(BF16)
    high = lines // LT
    half = high // 2
    channels = weight.shape[4]
    times, taps_high, taps_wide = weight.shape[:3]

    y = [{} for _ in range(LT)]
    wide = KW * high

    def multiply(frames, highs, first_time=True):
        if first_time and len(highs) % 2 == 0 and frames[-1] == LT - 1:
            partial([(0, kh) for kh in highs], frames[:-1])
            first_time = False
        partial([(kt, kh) for kh in highs for kt in range(times) if kt or (first_time and frames != (LT - 1,))], frames)

    def partial(taps, frames):
        for at in range(0, len(taps), 2):
            pair = taps[at:at + 2]
            for kw, (first, last) in enumerate(((0, 3), (1, 3), (1, 4))):
                tile = jnp.concatenate([weight[kt, kh, kw] for kt, kh in pair], axis=1)
                rows = [x[f * wide + first * high:f * wide + last * high] for f in frames]
                product = dot(jnp.concatenate(rows, axis=0), tile)
                for f in frames:
                    for which, (kt, kh) in enumerate(pair):
                        y[f][kt, kh, kw] = {}
                        for column in range(first, last):
                            start = ((f - frames[0]) * (last - first) + column - first) * high
                            y[f][kt, kh, kw][column] = product[start:start + high, which * channels:(which + 1) * channels]

    offset, mine1, other1, mine2, other2 = (params[pl.ds(at, 1), :] for at in range(5))

    def over_time(f, kh, kw, column):
        if f == 0:
            y0, y1, y2 = (y[0][kt, kh, kw][column] for kt in range(times))
            return [(y0 + y1) + y2]
        before0, before1 = (y[f - 1][kt, kh, kw][column] for kt in range(2))
        y1, y2 = (y[f][kt, kh, kw][column] for kt in (1, 2))
        return [(before0 + before1) + y2, before0 + (y1 + y2)]

    def add(*terms):
        return [functools.reduce(lambda a, b: a + b, parts) for parts in zip(*terms)]

    def stages(f):
        stage = []
        for kh in range(taps_high):
            k0 = {column: over_time(f, kh, 0, column) for column in (0, 1, 2)}
            k1 = {column: over_time(f, kh, 1, column) for column in (1, 2)}
            k2 = {column: over_time(f, kh, 2, column) for column in (1, 2, 3)}
            if kh == 1:
                k1 = {column: [v + offset for v in k1[column]] for column in k1}
            lower = add(k0[1], k1[1])
            upper = add(k1[2], k2[2])
            stage.append((
                add(k0[0], k1[1], k2[1]),
                lower, add(lower, k2[2]),
                upper, add(upper, k0[1]),
                add(k0[2], k1[2], k2[3]),
            ))
        return stage

    zero = jnp.zeros((1, channels), F32)

    def act(v):
        return v + v * jnp.tanh(v)

    row_step = 2 * WD
    frame = 2 * high * row_step
    copies = []
    def finish(f):
        stage = stages(f)
        for a in range(len(stage[0][0])):
            g = max(2 * f - 1, 0) + a
            for b in range(2):
                for odd in range(2):
                    d = []
                    for at in range(6):
                        z = [stage[kh][at][a] for kh in range(3)]
                        even0, even1, even2 = (v[:half] for v in z)
                        odd0, odd1, odd2 = (v[half:] for v in z)
                        if b == 0 and odd == 0:
                            v = (jnp.concatenate([zero, odd0[:-1]], axis=0) + even1) + even2
                        elif b == 0:
                            v = (even0 + odd1) + odd2
                        elif odd == 0:
                            v = (even0 + even1) + odd2
                        else:
                            v = (odd0 + odd1) + jnp.concatenate([even2[1:], zero], axis=0)
                        d.append(act(v))
                    values = (d[0], mine1 * d[2] + other1 * d[1], mine2 * d[4] + other2 * d[3], d[5])
                    for p, value in enumerate(values):
                        start = g * frame + (2 * odd + b) * row_step + p
                        spread[pl.ds(start, half, stride=4 * row_step), :] = value
            part = pl.ds(g * frame, frame)
            out[part, :] = spread[part, :].astype(BF16)
            for to in (0, 1) if g == 0 else (g + 1,):
                copies.append(pltpu.make_async_copy(out.at[part], out_hbm.at[pl.ds(to * frame, frame)], sem.at[to]))
                copies[-1].start()

    multiply(tuple(range(LT)), (0, 1))
    for frames in ((0, 1, 2), (3,)):
        multiply(frames, (2,))
        for f in frames:
            finish(f)
    for copy in copies:
        copy.wait()


def per_device(latent_rows, line_order, conv_weight, conv_bias, blend_table, blend_ids):
    n = lax.axis_size("tile")
    lines = line_order.shape[0]
    channels = latent_rows.shape[1]
    out_channels = conv_weight.shape[-1]
    lines_dev = lines // n
    block = 16 * -(-KW * lines_dev // 16)
    frame_rows = 2 * (lines // LT) * 2 * WD
    out_rows = 2 * LT * frame_rows
    hbm = pl.BlockSpec(memory_space=pltpu.HBM)
    vmem = pl.BlockSpec(memory_space=pltpu.VMEM)
    gathered = pl.pallas_call(
        functools.partial(gather_kernel, n, block, lines),
        out_shape=(
            jax.ShapeDtypeStruct((n, block, channels), BF16),
            jax.ShapeDtypeStruct((KW * lines, n * block), BF16),
            jax.ShapeDtypeStruct(conv_weight.shape, BF16),
            jax.ShapeDtypeStruct((8, out_channels), F32),
        ),
        in_specs=[hbm] * 6,
        out_specs=(vmem,) * 4,
        scratch_shapes=[
            pltpu.VMEM(latent_rows.shape, BF16),
            pltpu.VMEM((lines_dev * HEAD, channels), BF16),
            pltpu.VMEM((1, lines), jnp.int32),
            pltpu.VMEM((1, out_channels), F32),
            pltpu.SMEM(blend_table.shape, F32),
            pltpu.SMEM(blend_ids.shape, jnp.int32),
            pltpu.VMEM((n, block, channels), BF16),
            pltpu.SemaphoreType.DMA((6,)),
            pltpu.SemaphoreType.DMA((lines_dev,)),
            pltpu.SemaphoreType.DMA((n,)),
            pltpu.SemaphoreType.DMA((n,)),
            pltpu.SemaphoreType.REGULAR((n,)),
        ],
        compiler_params=pltpu.CompilerParams(collective_id=0, has_side_effects=True, vmem_limit_bytes=20 << 20),
    )(*(pltpu.with_memory_space_constraint(v, pltpu.HBM) for v in (
        latent_rows, line_order.reshape(1, lines), conv_weight,
        conv_bias.reshape(1, out_channels), blend_table, blend_ids)))
    out = pl.pallas_call(
        functools.partial(conv_kernel, lines),
        out_shape=jax.ShapeDtypeStruct((out_rows, out_channels), BF16),
        in_specs=[vmem] * 4,
        out_specs=hbm,
        scratch_shapes=[
            pltpu.VMEM((frame_rows * (2 * LT - 1), out_channels), F32),
            pltpu.VMEM((frame_rows * (2 * LT - 1), out_channels), BF16),
            pltpu.SemaphoreType.DMA((2 * LT,)),
        ],
        compiler_params=pltpu.CompilerParams(vmem_limit_bytes=20 << 20),
    )(*gathered)
    return out.reshape(2 * LT, 2 * (lines // LT), 2 * WD, out_channels)


def solution(mesh):
    return jax.shard_map(
        per_device,
        mesh=mesh,
        in_specs=(P(("groups", "tile"), None), P("groups"), P(), P(), P(), P("groups")),
        out_specs=P("groups", None, "tile", None),
        check_vma=False,
    )
```

```python
import functools

import jax
import jax.numpy as jnp
from jax import lax
from jax.experimental import pallas as pl
from jax.experimental.pallas import tpu as pltpu
from jax.sharding import PartitionSpec as P

LT = 4
WD = 2
KW = WD + 2
FIRST = 2
HEAD = 16
F32 = jnp.float32
BF16 = jnp.bfloat16
MESH = pl.DeviceIdType.MESH


def log2(n):
    assert n & (n - 1) == 0
    return n.bit_length() - 1


def iota(shape, dim):
    return lax.broadcasted_iota(jnp.int32, shape, dim)


def dot(a, b):
    return jnp.dot(a, b, preferred_element_type=F32)


def gather_kernel(n, block, lines,
                  rows_hbm, order_hbm, weight_hbm, bias_hbm, table_hbm, ids_hbm,
                  recv, sort, weight, params,
                  rows, head, order, bias, table, ids, send,
                  local_sem, head_sem, send_sem, recv_sem, ready_sem):
    me = lax.axis_index("tile")
    lines_dev = lines // n
    width = WD * n
    barrier = pltpu.get_barrier_semaphore()
    heads = [
        pltpu.make_async_copy(
            rows_hbm.at[pl.ds(line * width, HEAD)], head.at[pl.ds(line * HEAD, HEAD)], head_sem.at[line])
        for line in range(lines_dev)
    ]
    loads = [
        pltpu.make_async_copy(source, target, local_sem.at[at])
        for at, (source, target) in enumerate((
            (rows_hbm, rows), (order_hbm, order), (bias_hbm, bias),
            (table_hbm, table), (ids_hbm, ids), (weight_hbm, weight)))
    ]
    for load in heads:
        load.start()
    loads[0].start()

    def enter(j, carry):
        pl.semaphore_signal(barrier, inc=1, device_id={"tile": j}, device_id_type=MESH)
        return carry

    lax.fori_loop(me + 1, n, enter, 0)
    for load in loads[1:]:
        load.start()

    def pick(count, first, pitch):
        shape = (count * block, lines_dev * pitch)
        at = iota(shape, 0)
        inside = at & (block - 1)
        column = (inside >> log2(lines_dev)) + ((at >> log2(block)) + first) * WD - 1
        line = inside & (lines_dev - 1)
        chosen = (iota(shape, 1) == line * pitch + column) & (column >= 0) & (column < width) & (inside < KW * lines_dev)
        return jnp.where(chosen, 1.0, 0.0).astype(BF16)

    def copy_to(peer):
        return pltpu.make_async_remote_copy(
            src_ref=send.at[peer], dst_ref=recv.at[me],
            send_sem=send_sem.at[peer], recv_sem=recv_sem.at[me],
            device_id={"tile": peer}, device_id_type=MESH)

    pick_head = pick(FIRST - 1, 1, HEAD)
    pick_rest = pick(n - FIRST, FIRST, width)
    def answer(j, carry):
        pl.semaphore_signal(ready_sem.at[me], inc=1, device_id={"tile": j}, device_id_type=MESH)
        return carry

    @pl.when(me > 0)
    def _():
        pl.semaphore_wait(barrier, me)
        answer(0, 0)

    for load in heads:
        load.wait()
    near = head[...].astype(F32)
    pieces = [near[line * HEAD:line * HEAD + KW] for line in range(lines_dev)]
    if block > KW * lines_dev:
        pieces.append(jnp.zeros((block - KW * lines_dev, near.shape[1]), F32))
    send[0] = jnp.concatenate(pieces, axis=0).astype(BF16)

    @pl.when(me > 0)
    def _():
        copy_to(0).start()

    send[pl.ds(1, FIRST - 1)] = dot(pick_head, head[...]).astype(BF16).reshape(FIRST - 1, block, -1)
    for j in range(1, FIRST):
        @pl.when(j < me)
        def _():
            copy_to(j).start()

    lax.fori_loop(1, me, answer, 0)

    loads[0].wait()
    send[pl.ds(FIRST, n - FIRST)] = dot(pick_rest, rows[...]).astype(BF16).reshape(n - FIRST, block, -1)
    pltpu.make_async_copy(send.at[me], recv.at[me], recv_sem.at[me]).start()

    def send_lower(j, carry):
        copy_to(j).start()
        return carry

    def send_higher(j, carry):
        pl.semaphore_wait(ready_sem.at[j], 1)
        copy_to(j).start()
        return carry

    lax.fori_loop(FIRST, me, send_lower, 0)
    lax.fori_loop(me + 1, n, send_higher, 0)

    loads[1].wait()
    received = n * block

    def entry(shape, dim):
        at = iota(shape, dim)
        inside = at & (block - 1)
        by_line = me == 0
        line = jnp.where(by_line, inside >> log2(KW), inside & (lines_dev - 1))
        column = jnp.where(by_line, (inside & (KW - 1)) + 1, inside >> log2(lines_dev))
        valid = (inside < KW * lines_dev) & (column < KW)
        return (at >> log2(block)) * lines_dev + line, column, valid

    shape = (lines, received)
    position, _, valid = entry(shape, 1)
    expand = jnp.where((iota(shape, 0) == position) & valid, 1.0, 0.0).astype(BF16)
    held = jnp.broadcast_to(order[...].astype(F32), (8, lines)).astype(BF16)
    line_of = dot(held, expand)[:1].astype(jnp.int32)
    high = lines // LT
    row = line_of & (high - 1)
    line_of = (line_of - row) * KW + (row & 1) * (high // 2) + (row >> 1)
    _, column, valid = entry((1, received), 1)
    slot = jnp.where(valid, column * high + line_of, -1)
    sort[...] = jnp.where(iota((KW * lines, received), 0) == slot, 0.5, 0.0).astype(BF16)

    for load in loads[2:]:
        load.wait()

    def profile(tile):
        kind = ids[tile]
        return [jnp.full((1, 128), table[kind, c], F32) for c in range(4 * WD)]

    has_lower = jnp.where(me > 0, 1.0, 0.0)
    has_upper = jnp.where(me < n - 1, 1.0, 0.0)
    mine = profile(me)[3:-3]
    other = [profile(jnp.maximum(me - 1, 0))[-1] * has_lower, profile(jnp.minimum(me + 1, n - 1))[0] * has_upper]
    for p in range(2):
        total = mine[p] + other[p]
        params[pl.ds(2 * p + 1, 1), :] = mine[p] / total
        params[pl.ds(2 * p + 2, 1), :] = other[p] / total
    params[pl.ds(0, 1), :] = 0.5 * bias[...]

    def sent_to(k, carry):
        copy_to(lax.rem(me + k, n)).wait_send()
        return carry

    lax.fori_loop(1, n, sent_to, 0)

    for j in range(n):
        pltpu.make_async_copy(send.at[j], recv.at[j], recv_sem.at[j]).wait()


def conv_kernel(lines, recv, sort, weight, params, out_hbm, spread, out, sem):
    x = dot(sort[...], recv[...].reshape(sort.shape[1], recv.shape[2])).astype(BF16)
    high = lines // LT
    half = high // 2
    channels = weight.shape[4]
    times, taps_high, taps_wide = weight.shape[:3]

    y = [{} for _ in range(LT)]
    wide = KW * high

    def multiply(frames, highs, first_time=True):
        if first_time and len(highs) % 2 == 0 and frames[-1] == LT - 1:
            partial([(0, kh) for kh in highs], frames[:-1])
            first_time = False
        partial([(kt, kh) for kh in highs for kt in range(times) if kt or (first_time and frames != (LT - 1,))], frames)

    def partial(taps, frames):
        outer = [(0, 0, 3), (2, 1, 4), (1, 1, 3)]
        work = [(first, last, [(*tap, kw) for tap in taps[at:at + 2]])
                for at in range(0, len(taps) - 1, 2) for kw, first, last in outer]
        if len(taps) % 2:
            work += [(0, KW, [(*taps[-1], 0), (*taps[-1], 2)]), (1, 3, [(*taps[-1], 1)])]
        for first, last, pair in work:
            tile = jnp.concatenate([weight[tap] for tap in pair], axis=1)
            rows = [x[f * wide + first * high:f * wide + last * high] for f in frames]
            product = dot(jnp.concatenate(rows, axis=0), tile)
            for f in frames:
                for which, tap in enumerate(pair):
                    y[f][tap] = {}
                    for column in range(first, last):
                        start = ((f - frames[0]) * (last - first) + column - first) * high
                        y[f][tap][column] = product[start:start + high, which * channels:(which + 1) * channels]

    offset, mine1, other1, mine2, other2 = (params[pl.ds(at, 1), :] for at in range(5))

    def over_time(f, kh, kw, column):
        if f == 0:
            y0, y1, y2 = (y[0][kt, kh, kw][column] for kt in range(times))
            return [(y0 + y1) + y2]
        before0, before1 = (y[f - 1][kt, kh, kw][column] for kt in range(2))
        y1, y2 = (y[f][kt, kh, kw][column] for kt in (1, 2))
        return [(before0 + before1) + y2, before0 + (y1 + y2)]

    def add(*terms):
        return [functools.reduce(lambda a, b: a + b, parts) for parts in zip(*terms)]

    def stages(f):
        stage = []
        for kh in range(taps_high):
            k0 = {column: over_time(f, kh, 0, column) for column in (0, 1, 2)}
            k1 = {column: over_time(f, kh, 1, column) for column in (1, 2)}
            k2 = {column: over_time(f, kh, 2, column) for column in (1, 2, 3)}
            if kh == 1:
                k1 = {column: [v + offset for v in k1[column]] for column in k1}
            lower = add(k0[1], k1[1])
            upper = add(k1[2], k2[2])
            stage.append((
                add(k0[0], k1[1], k2[1]),
                lower, add(lower, k2[2]),
                upper, add(upper, k0[1]),
                add(k0[2], k1[2], k2[3]),
            ))
        return stage

    zero = jnp.zeros((1, channels), F32)

    def act(v):
        return v + v * jnp.tanh(v)

    row_step = 2 * WD
    frame = 2 * high * row_step
    copies = []
    def finish(f):
        stage = stages(f)
        for a in range(len(stage[0][0])):
            g = max(2 * f - 1, 0) + a
            for b in range(2):
                for odd in range(2):
                    d = []
                    for at in range(6):
                        z = [stage[kh][at][a] for kh in range(3)]
                        even0, even1, even2 = (v[:half] for v in z)
                        odd0, odd1, odd2 = (v[half:] for v in z)
                        if b == 0 and odd == 0:
                            v = (jnp.concatenate([zero, odd0[:-1]], axis=0) + even1) + even2
                        elif b == 0:
                            v = (even0 + odd1) + odd2
                        elif odd == 0:
                            v = (even0 + even1) + odd2
                        else:
                            v = (odd0 + odd1) + jnp.concatenate([even2[1:], zero], axis=0)
                        d.append(act(v))
                    values = (d[0], mine1 * d[2] + other1 * d[1], mine2 * d[4] + other2 * d[3], d[5])
                    for p, value in enumerate(values):
                        start = g * frame + (2 * odd + b) * row_step + p
                        spread[pl.ds(start, half, stride=4 * row_step), :] = value
            part = pl.ds(g * frame, frame)
            out[part, :] = spread[part, :].astype(BF16)
            for to in (0, 1) if g == 0 else (g + 1,):
                copies.append(pltpu.make_async_copy(out.at[part], out_hbm.at[pl.ds(to * frame, frame)], sem.at[to]))
                copies[-1].start()

    multiply(tuple(range(LT)), (0, 1))
    for frames in ((0, 1, 2), (3,)):
        multiply(frames, (2,))
        for f in frames:
            finish(f)
    for copy in copies:
        copy.wait()


def per_device(latent_rows, line_order, conv_weight, conv_bias, blend_table, blend_ids):
    n = lax.axis_size("tile")
    lines = line_order.shape[0]
    channels = latent_rows.shape[1]
    out_channels = conv_weight.shape[-1]
    lines_dev = lines // n
    block = 16 * -(-KW * lines_dev // 16)
    frame_rows = 2 * (lines // LT) * 2 * WD
    out_rows = 2 * LT * frame_rows
    hbm = pl.BlockSpec(memory_space=pltpu.HBM)
    vmem = pl.BlockSpec(memory_space=pltpu.VMEM)
    gathered = pl.pallas_call(
        functools.partial(gather_kernel, n, block, lines),
        out_shape=(
            jax.ShapeDtypeStruct((n, block, channels), BF16),
            jax.ShapeDtypeStruct((KW * lines, n * block), BF16),
            jax.ShapeDtypeStruct(conv_weight.shape, BF16),
            jax.ShapeDtypeStruct((8, out_channels), F32),
        ),
        in_specs=[hbm] * 6,
        out_specs=(vmem,) * 4,
        scratch_shapes=[
            pltpu.VMEM(latent_rows.shape, BF16),
            pltpu.VMEM((lines_dev * HEAD, channels), BF16),
            pltpu.VMEM((1, lines), jnp.int32),
            pltpu.VMEM((1, out_channels), F32),
            pltpu.SMEM(blend_table.shape, F32),
            pltpu.SMEM(blend_ids.shape, jnp.int32),
            pltpu.VMEM((n, block, channels), BF16),
            pltpu.SemaphoreType.DMA((6,)),
            pltpu.SemaphoreType.DMA((lines_dev,)),
            pltpu.SemaphoreType.DMA((n,)),
            pltpu.SemaphoreType.DMA((n,)),
            pltpu.SemaphoreType.REGULAR((n,)),
        ],
        compiler_params=pltpu.CompilerParams(collective_id=0, has_side_effects=True, vmem_limit_bytes=20 << 20),
    )(*(pltpu.with_memory_space_constraint(v, pltpu.HBM) for v in (
        latent_rows, line_order.reshape(1, lines), conv_weight,
        conv_bias.reshape(1, out_channels), blend_table, blend_ids)))
    out = pl.pallas_call(
        functools.partial(conv_kernel, lines),
        out_shape=jax.ShapeDtypeStruct((out_rows, out_channels), BF16),
        in_specs=[vmem] * 4,
        out_specs=hbm,
        scratch_shapes=[
            pltpu.VMEM((frame_rows * (2 * LT - 1), out_channels), F32),
            pltpu.VMEM((frame_rows * (2 * LT - 1), out_channels), BF16),
            pltpu.SemaphoreType.DMA((2 * LT,)),
        ],
        compiler_params=pltpu.CompilerParams(vmem_limit_bytes=20 << 20),
    )(*gathered)
    return out.reshape(2 * LT, 2 * (lines // LT), 2 * WD, out_channels)


def solution(mesh):
    return jax.shard_map(
        per_device,
        mesh=mesh,
        in_specs=(P(("groups", "tile"), None), P("groups"), P(), P(), P(), P("groups")),
        out_specs=P("groups", None, "tile", None),
        check_vma=False,
    )
```
